32 devices in a mesh: row: 8 (over z, x), col: 4 (over y, core).
Axes of the slice: x: 2, y: 2, z: 4, core: 2. Of those that a mesh axis runs over, the one named last changes fastest.
Arguments:
- subspace: bfloat16 [256, 32768], P('col', 'row'), may hold values from -400 to 400
- onsite: float32 [32768], P('row'), may hold values from -1.5 to 1.5
- blocks: bfloat16 [20, 256, 128, 128], P(None, 'row'), may hold values from -0.125 to 0.125
- cols: int32 [256, 20], replicated, may hold values from 0 to 255, as said below
Outputs:
- basis: float32 [256, 32768], P('col', 'row')
- factor: float32 [256, 256], replicated
The draws below stay inside these ranges and needn't reach their ends.
Inputs may be any that keep to these rules, and one draw needn't show every extreme that they name: `cols`: the block rows are numbered by device: device r of row holds block rows r * 32 to (r + 1) * 32 - 1. A block row names block rows of its own device or of the devices r + 1, r - 1, r + 2 and r + 4 along row, counted round. The block rows of one device name between 1 and 4 distinct block rows of each of these four devices, and in every draw some device names exactly 4 on each of its four.
All inputs are finite; a program needn't handle non-finite values.
Results may differ from the reference program's by a relative error of at most 0.0044.
Values may be sent and summed in bfloat16 or wider, within the bound.
A program may use at most 128 MiB of HBM per device.

```python
import math
import jax
import jax.numpy as jnp
from jax import lax

BS = 128
NNZ = 20
S = 256
HALO = 4
FILTER = 4
BR_DEV = 32
NB = 256
NTOT = 32768


remote_slots = 4


def draw_cols(key, part):
    row_count = NB // BR_DEV
    keys = jax.random.split(jax.random.fold_in(key, 7), 5)
    counts = jax.random.randint(keys[0], (row_count, 4), 1, HALO + 1)
    busiest = jax.random.randint(keys[1], (), 0, row_count)
    counts = jnp.where(jnp.arange(row_count)[:, None] == busiest, HALO, counts)
    scores = jax.random.randint(keys[2], (row_count, 4, BR_DEV), 0, 2 ** 20) * BR_DEV + jnp.arange(BR_DEV)
    orders = jnp.argsort(scores, axis=-1).astype(jnp.int32)
    local_rows = jnp.arange(BR_DEV)[:, None]
    slot_ids = jnp.arange(NNZ)[None, :]
    pair_ids = (local_rows * remote_slots + slot_ids) % (4 * HALO)
    group_ids = pair_ids // HALO
    member_ids = pair_ids % HALO
    device_ids = jnp.arange(row_count)[:, None, None]
    valid = (slot_ids < remote_slots)[None] & (member_ids[None] < counts[device_ids, group_ids[None]])
    offsets = jnp.array([1, -1, 2, row_count // 2], dtype=jnp.int32)
    owners = (device_ids + offsets[group_ids][None]) % row_count
    chosen = orders[device_ids, group_ids[None], member_ids[None]]
    remote = owners * BR_DEV + chosen
    local = jax.random.randint(keys[3], (row_count, BR_DEV, NNZ), 0, BR_DEV) + device_ids * BR_DEV
    named = jnp.where(valid, remote, local)
    slot_scores = jax.random.randint(keys[4], (row_count, BR_DEV, NNZ), 0, 2 ** 20) * NNZ + jnp.arange(NNZ)
    slot_order = jnp.argsort(slot_scores, axis=-1)
    named = jnp.take_along_axis(named, slot_order, axis=-1)
    return named.reshape(NB, NNZ).astype(jnp.int32)


def draw_subspace(key, part):
    keys = jax.random.split(jax.random.fold_in(key, 11), 3)
    values = jax.random.normal(keys[0], (S, NTOT), jnp.float32)
    column_scale = jnp.exp(jax.random.uniform(keys[1], (S, 1), jnp.float32) * math.log(10.0))
    row_scale = jnp.exp(jax.random.uniform(keys[2], (1, NTOT), jnp.float32) * math.log(10.0))
    row_scale = row_scale * 3.0 ** (jnp.arange(NTOT, dtype=jnp.float32)[None, :] / NTOT)
    return (0.1 * values * column_scale * row_scale).astype(jnp.bfloat16)


def level_of(stream_key, dims, cuts, smallest, largest):
    def one(axis_at, blocks):
        draws = jax.random.uniform(jax.random.fold_in(jax.random.fold_in(stream_key, 6), axis_at), (blocks,), jnp.float32, smallest / len(cuts), largest / len(cuts))
        return jnp.repeat(jnp.exp(draws), dims[axis_at] // blocks).reshape((-1,) + (1,) * (len(dims) - axis_at - 1))

    loudness = one(*cuts[0])
    for cut in cuts[1:]:
        loudness = loudness * one(*cut)
    return loudness


def noise(key, extent, deviation, bound, cuts=(), kind=jnp.bfloat16):
    level = level_of(key, extent, cuts, -0.22, 0.18) if cuts else 1.0
    entries = jax.random.normal(key, extent, jnp.float32) * deviation * level
    return jnp.minimum(jnp.maximum(entries, -bound), bound).astype(kind)


def setup_inputs(seed: int = 0) -> dict:
    key_list = jax.random.split(jax.random.key(seed), 5)
    subspace = draw_subspace(jax.random.fold_in(key_list[4], 71), 0)
    onsite = jnp.clip(jax.random.uniform(key_list[1], (NTOT,), jnp.float32, -1.5, 1.5) * level_of(key_list[1], (NTOT,), ((0, 8),), -0.4, 0.0), -1.5, 1.5)
    blocks = noise(key_list[2], (NNZ, NB, BS, BS), (NNZ * BS) ** -0.5, 0.125, ((1, 8),))
    cols = draw_cols(jax.random.fold_in(key_list[4], 71), 0)
    return {"subspace": subspace, "onsite": onsite, "blocks": blocks, "cols": cols}


filter_scale = 0.4

def couple(lowered, onsite, blocks, cols):
    shaped = lowered.reshape(S, NB, BS)

    def add_slot(total, pair):
        slot_cols, slot_blocks = pair
        taken = jnp.take(shaped, slot_cols, axis=1).astype(jnp.float32)
        return (total + jnp.einsum('cla,lab->clb', taken, slot_blocks.astype(jnp.float32)), None)
    total, _ = lax.scan(add_slot, jnp.zeros((S, NB, BS), jnp.float32), (cols.T, blocks))
    return total.reshape(S, NTOT) + onsite[None, :] * lowered.astype(jnp.float32)

def reference(subspace, onsite, blocks, cols):
    previous = subspace.astype(jnp.float32)
    current = filter_scale * couple(subspace, onsite, blocks, cols)
    for filter_step in range(FILTER - 1):
        lowered = current.astype(jnp.bfloat16)
        following = 2.0 * filter_scale * couple(lowered, onsite, blocks, cols) - previous
        previous, current = (current, following)
    final = current.astype(jnp.bfloat16)
    gram = jnp.dot(final.astype(jnp.float32), final.T.astype(jnp.float32), preferred_element_type=jnp.float32)
    lower = jnp.linalg.cholesky(gram)
    inverse = lax.linalg.triangular_solve(lower, jnp.eye(S, dtype=jnp.float32), left_side=True, lower=True)
    basis = math.sqrt(NTOT) * jnp.dot(inverse, final.astype(jnp.float32), precision=lax.Precision.HIGHEST)
    factor = lower.T / math.sqrt(NTOT)
    return (basis, factor)
```

```python
import math

import jax
import jax.numpy as jnp
from jax import lax
from jax.experimental import pallas as pl
from jax.experimental.pallas import tpu as pltpu
from jax.sharding import PartitionSpec as P

HALO = 4
FILTER = 4
UNROLL = 4
filter_scale = 0.4
f32 = jnp.float32
bf16 = jnp.bfloat16


def shifts_of(rows):
    return (rows // 2, 2, 1, -1)


def index_tables(cols, rows, me, lb):
    sc = cols.shape[1]
    shifts = shifts_of(rows)
    groups = len(shifts)
    own = lax.dynamic_slice_in_dim(cols, me * lb, lb, 0).reshape(-1)
    askers = [
        lax.dynamic_slice_in_dim(cols, lax.rem(me - d + rows, rows) * lb, lb, 0).reshape(-1)
        for d in shifts
    ]
    owners = jnp.stack([lax.rem(me + d + rows, rows) for d in shifts])
    k = jnp.arange(lb, dtype=jnp.int32)
    wanted = own[None, :] - owners[:, None] * lb
    asked = jnp.stack(askers) - me * lb
    rel = jnp.concatenate([wanted, asked], 0)
    hit = jnp.any(rel[:, :, None] == k, axis=1)
    before = (k[:, None] < k[None, :])
    rank = jnp.sum((hit[:, :, None] & before[None]).astype(jnp.int32), axis=1)
    hit_e, rank_e = hit[groups:], rank[groups:]
    g = jnp.arange(groups, dtype=jnp.int32)
    key = jnp.min(jnp.where(hit_e, g[:, None], groups), axis=0)
    ahead = (key[:, None] < key[None, :]) | ((key[:, None] == key[None, :]) & before)
    inv = jnp.sum(ahead.astype(jnp.int32), axis=0)
    perm = jnp.sum(jnp.where(inv[None, :] == k[:, None], k[None, :], 0), axis=1)
    m = jnp.arange(HALO, dtype=jnp.int32)
    pick = hit_e[:, None, :] & (rank_e[:, None, :] == m[:, None])
    exp_n = jnp.sum(jnp.where(pick, k, 0), axis=-1)
    exp_p = jnp.sum(jnp.where(pick, inv, 0), axis=-1)
    slot = lb + HALO * g[:, None] + rank[:groups]
    match = wanted[:, :, None] == k
    far = jnp.sum(jnp.where(match, slot[:, None, :], 0), axis=(0, 2))
    near = own - me * lb
    mine = (near >= 0) & (near < lb)
    near_p = jnp.sum(jnp.where(near[:, None] == k, inv, 0), axis=1)
    pos_n = jnp.where(mine, near, far)
    pos_p = jnp.where(mine, near_p, far)
    return jnp.concatenate(
        [pos_n, pos_p, perm, inv, exp_n.reshape(-1), exp_p.reshape(-1)]
    ).astype(jnp.int32)


def filter_kernel(rows, lb, sc, tab, sub, ons, blk, out, bm, x0, x1, x2, x3, s0, y1, y2, y3,
                  snd0, snd1, snd2, snd3, bsem, xsem, csem, ssem, rsem):
    me = lax.axis_index("row")
    shifts = shifts_of(rows)
    groups = len(shifts)
    pn, pp = 0, lb * sc
    pperm = 2 * lb * sc
    pinv = pperm + lb
    pexn = pinv + lb
    pexp = pexn + groups * HALO
    xs, snds = (x0, x1, x2, x3), (snd0, snd1, snd2, snd3)
    bs = blk.shape[-1]
    chunks = lb // UNROLL

    def load(c):
        part = pl.ds(c * UNROLL, UNROLL)
        return pltpu.make_async_copy(blk.at[:, part], bm.at[:, part], bsem.at[c])

    def first(i):
        cut = pl.ds(pl.multiple_of(i * bs, bs), bs)
        return (pltpu.make_async_copy(sub.at[:, cut], x0.at[i], xsem.at[i]),
                pltpu.make_async_copy(sub.at[:, cut], s0.at[i], csem.at[i]))

    @pl.loop(0, lb)
    def _(i):
        a, b = first(i)
        b.start()
        a.start()

    @pl.loop(0, chunks)
    def _(c):
        load(c).start()

    barrier = pltpu.get_barrier_semaphore()
    for d in shifts:
        pl.semaphore_signal(barrier, inc=1, device_id={"row": lax.rem(me + d + rows, rows)},
                            device_id_type=pl.DeviceIdType.MESH)

    def copy(k, g):
        return pltpu.make_async_remote_copy(
            src_ref=snds[k].at[pl.ds(g * HALO, HALO)],
            dst_ref=xs[k].at[pl.ds(lb + g * HALO, HALO)],
            send_sem=ssem.at[k, g], recv_sem=rsem.at[k, g],
            device_id={"row": lax.rem(me - shifts[g] + rows, rows)},
            device_id_type=pl.DeviceIdType.MESH)

    def pack(k, g, source, base):
        for m in range(HALO):
            snds[k][g * HALO + m] = source[tab[base + g * HALO + m]].astype(bf16)

    @pl.loop(0, lb)
    def _(i):
        first(i)[1].wait()

    for g in range(groups):
        pack(0, g, s0, pexn)
    pl.semaphore_wait(barrier, groups)

    @pl.loop(0, lb)
    def _(i):
        first(i)[0].wait()

    for g in range(groups):
        copy(0, g).start()

    def product(k, j):
        i = tab[pperm + j] if k in (1, 2) else j
        own = {0: j, 1: i, 2: j, 3: tab[pinv + j]}[k]
        base = pn if k < 2 else pp
        x = xs[k]
        left = jnp.concatenate([x[tab[base + i * sc + s]] for s in range(sc)], axis=1)
        right = jnp.concatenate([bm[s, i] for s in range(sc)], axis=0)
        acc = jnp.dot(left, right, preferred_element_type=f32)
        total = acc + ons[i] * x[own].astype(f32)
        if k == 0:
            return filter_scale * total
        prev = x0[i].astype(f32) if k == 1 else (y1[i] if k == 2 else y2[own])
        return 2.0 * filter_scale * total - prev

    for k in range(FILTER):
        for g in range(groups):
            copy(k, g).wait_recv()
        ys = (y1, y2, y3, None)[k]

        @pl.loop(0, chunks)
        def _(c):
            if k == 0:
                load(c).wait()
            if k in (1, 2):
                for g in range(groups):
                    @pl.when(c == g + 1)
                    def _():
                        pack(k + 1, g, ys, pexp)
            for u in range(UNROLL):
                j = c * UNROLL + u
                value = product(k, j)
                low = value.astype(bf16)
                if k < FILTER - 1:
                    xs[k + 1][j] = low
                    ys[j] = value
                else:
                    out[j] = low
                if k in (1, 2) and u == 1:
                    for g in range(groups):
                        @pl.when(c == g + 1)
                        def _():
                            copy(k + 1, g).start()

        if k == 0:
            for g in range(groups):
                pack(1, g, ys, pexn)
            for g in range(groups):
                copy(1, g).start()

    for k in range(FILTER):
        for g in range(groups):
            copy(k, g).wait_send()


def filtered(subspace, onsite, blocks, cols):
    rows = lax.axis_size("row")
    me = lax.axis_index("row")
    width = subspace.shape[0]
    sc, lb, bs, _ = blocks.shape
    groups = len(shifts_of(rows))
    tab = index_tables(cols, rows, me, lb)
    ext = lb + groups * HALO
    vm, dma = pltpu.VMEM, pltpu.SemaphoreType.DMA
    import functools
    return pl.pallas_call(
        functools.partial(filter_kernel, rows, lb, sc),
        out_shape=jax.ShapeDtypeStruct((lb, width, bs), bf16),
        in_specs=[pl.BlockSpec(memory_space=pltpu.SMEM), pl.BlockSpec(memory_space=pl.ANY),
                  pl.BlockSpec(memory_space=pltpu.VMEM), pl.BlockSpec(memory_space=pl.ANY)],
        out_specs=pl.BlockSpec(memory_space=pltpu.VMEM),
        scratch_shapes=[vm((sc, lb, bs, bs), bf16)]
        + [vm((ext, width, bs), bf16)] * 4
        + [vm((lb, width, bs), bf16)]
        + [vm((lb, width, bs), f32)] * 3
        + [vm((groups * HALO, width, bs), bf16)] * 4
        + [dma((lb // UNROLL,)), dma((lb,)), dma((lb,)), dma((FILTER, groups)), dma((FILTER, groups))],
        compiler_params=pltpu.CompilerParams(
            collective_id=0, has_side_effects=True, vmem_limit_bytes=56 * 1024 * 1024),
        name="filter",
    )(tab, subspace, onsite.reshape(lb, 1, bs), blocks)


def body(subspace, onsite, blocks, cols):
    row_count = lax.axis_size("row")
    part_width, local_rows = subspace.shape
    final = filtered(subspace, onsite, blocks, cols)
    final = jnp.transpose(final, (1, 0, 2)).reshape(part_width, local_rows)
    S = part_width * lax.axis_size("col")
    whole = lax.all_gather(final, "col", axis=0, tiled=True)
    gram_local = jnp.einsum("ar,br->ab", whole, whole, preferred_element_type=jnp.float32)
    gram = lax.psum(gram_local, "row")
    lower = jnp.linalg.cholesky(gram)
    total_rows = row_count * local_rows
    inverse = lax.linalg.triangular_solve(
        lower, jnp.eye(S, dtype=jnp.float32), left_side=True, lower=True
    )
    own_part = lax.dynamic_slice_in_dim(inverse, lax.axis_index("col") * part_width, part_width, 0)
    basis = math.sqrt(total_rows) * jnp.dot(
        own_part, whole.astype(jnp.float32), precision=lax.Precision.HIGHEST
    )
    factor = lower.T / math.sqrt(total_rows)
    return (basis, factor)


def solution(mesh):
    in_specs = (P("col", "row"), P("row"), P(None, "row", None, None), P())
    out_specs = (P("col", "row"), P())
    return jax.shard_map(body, mesh=mesh, in_specs=in_specs, out_specs=out_specs, check_vma=False)
```

```python
import functools
import math

import jax
import jax.numpy as jnp
from jax import lax
from jax.experimental import pallas as pl
from jax.experimental.pallas import tpu as pltpu
from jax.sharding import PartitionSpec as P

HALO = 4
FILTER = 4
UNROLL = 4
filter_scale = 0.4
f32 = jnp.float32
bf16 = jnp.bfloat16


def shifts_of(rows):
    return (rows // 2, 2, 1, -1)


def index_tables(cols, rows, me, lb):
    sc = cols.shape[1]
    shifts = shifts_of(rows)
    groups = len(shifts)
    own = lax.dynamic_slice_in_dim(cols, me * lb, lb, 0).reshape(-1)
    askers = [
        lax.dynamic_slice_in_dim(cols, lax.rem(me - d + rows, rows) * lb, lb, 0).reshape(-1)
        for d in shifts
    ]
    owners = jnp.stack([lax.rem(me + d + rows, rows) for d in shifts])
    k = jnp.arange(lb, dtype=jnp.int32)
    wanted = own[None, :] - owners[:, None] * lb
    asked = jnp.stack(askers) - me * lb
    rel = jnp.concatenate([wanted, asked], 0)
    hit = jnp.any(rel[:, :, None] == k, axis=1)
    before = (k[:, None] < k[None, :])
    rank = jnp.sum((hit[:, :, None] & before[None]).astype(jnp.int32), axis=1)
    hit_e, rank_e = hit[groups:], rank[groups:]
    g = jnp.arange(groups, dtype=jnp.int32)
    key = jnp.min(jnp.where(hit_e, g[:, None], groups), axis=0)
    ahead = (key[:, None] < key[None, :]) | ((key[:, None] == key[None, :]) & before)
    inv = jnp.sum(ahead.astype(jnp.int32), axis=0)
    perm = jnp.sum(jnp.where(inv[None, :] == k[:, None], k[None, :], 0), axis=1)
    m = jnp.arange(HALO, dtype=jnp.int32)
    pick = hit_e[:, None, :] & (rank_e[:, None, :] == m[:, None])
    exp_n = jnp.sum(jnp.where(pick, k, 0), axis=-1)
    exp_p = jnp.sum(jnp.where(pick, inv, 0), axis=-1)
    slot = lb + HALO * g[:, None] + rank[:groups]
    match = wanted[:, :, None] == k
    far = jnp.sum(jnp.where(match, slot[:, None, :], 0), axis=(0, 2))
    near = own - me * lb
    mine = (near >= 0) & (near < lb)
    near_p = jnp.sum(jnp.where(near[:, None] == k, inv, 0), axis=1)
    pos_n = jnp.where(mine, near, far)
    pos_p = jnp.where(mine, near_p, far)
    return jnp.concatenate(
        [pos_n, pos_p, perm, inv, exp_n.reshape(-1), exp_p.reshape(-1)]
    ).astype(jnp.int32)


def flip(c, bit):
    return c + bit - 2 * bit * lax.rem(c // bit, 2)


def hops_of(parts):
    hops, held, bit = [], [0], parts // 2
    while bit:
        hops += [(bit, m) for m in held]
        held += [m + bit for m in held]
        bit //= 2
    return hops


def slice_of(width, rows):
    return max(8, width // rows)


def filter_kernel(rows, parts, lb, sc, tab, sub, ons, blk, out, gram, bm, x0, x1, x2, x3, s0, y1, y2, y3,
                  snd0, snd1, snd2, snd3, gp, gs, rb, bsem, xsem, csem, ssem, rsem,
                  wss, wrs, pss, prs, ass, ars):
    me = lax.axis_index("row")
    mc = lax.axis_index("col")
    everyone = rows * parts
    linear = me * parts + mc
    width = out.shape[2]
    hops = hops_of(parts)
    rps = slice_of(width, rows)
    reducers = width // rps
    shifts = shifts_of(rows)
    groups = len(shifts)
    pn, pp = 0, lb * sc
    pperm = 2 * lb * sc
    pinv = pperm + lb
    pexn = pinv + lb
    pexp = pexn + groups * HALO
    xs, snds = (x0, x1, x2, x3), (snd0, snd1, snd2, snd3)
    bs = blk.shape[-1]
    chunks = lb // UNROLL

    def load(c):
        part = pl.ds(c * UNROLL, UNROLL)
        return pltpu.make_async_copy(blk.at[:, part], bm.at[:, part], bsem.at[c])

    def first(i):
        cut = pl.ds(pl.multiple_of(i * bs, bs), bs)
        return (pltpu.make_async_copy(sub.at[:, cut], x0.at[i], xsem.at[i]),
                pltpu.make_async_copy(sub.at[:, cut], s0.at[i], csem.at[i]))

    @pl.loop(0, lb)
    def _(i):
        a, b = first(i)
        b.start()
        a.start()

    @pl.loop(0, chunks)
    def _(c):
        load(c).start()

    barrier = pltpu.get_barrier_semaphore()

    @pl.loop(1, everyone)
    def _(e):
        to = lax.rem(linear + e, everyone)
        pl.semaphore_signal(barrier, inc=1, device_id=(to // parts, lax.rem(to, parts)),
                            device_id_type=pl.DeviceIdType.MESH)

    def copy(k, g):
        return pltpu.make_async_remote_copy(
            src_ref=snds[k].at[pl.ds(g * HALO, HALO)],
            dst_ref=xs[k].at[pl.ds(lb + g * HALO, HALO)],
            send_sem=ssem.at[k, g], recv_sem=rsem.at[k, g],
            device_id=(lax.rem(me - shifts[g] + rows, rows), mc),
            device_id_type=pl.DeviceIdType.MESH)

    def pack(k, g, source, base):
        for m in range(HALO):
            snds[k][g * HALO + m] = source[tab[base + g * HALO + m]].astype(bf16)

    @pl.loop(0, lb)
    def _(i):
        first(i)[1].wait()

    for g in range(groups):
        pack(0, g, s0, pexn)
    pl.semaphore_wait(barrier, everyone - 1)

    @pl.loop(0, lb)
    def _(i):
        first(i)[0].wait()

    for g in range(groups):
        copy(0, g).start()

    def product(k, j):
        i = tab[pperm + j] if k in (1, 2) else j
        own = {0: j, 1: i, 2: j, 3: tab[pinv + j]}[k]
        base = pn if k < 2 else pp
        x = xs[k]
        left = jnp.concatenate([x[tab[base + i * sc + s]] for s in range(sc)], axis=1)
        right = jnp.concatenate([bm[s, i] for s in range(sc)], axis=0)
        acc = jnp.dot(left, right, preferred_element_type=f32)
        total = acc + ons[i] * x[own].astype(f32)
        if k == 0:
            return filter_scale * total
        prev = x0[i].astype(f32) if k == 1 else (y1[i] if k == 2 else y2[own])
        return 2.0 * filter_scale * total - prev

    def spread(h, c):
        bit, m = hops[h]
        piece = mc
        for b in (m & (1 << t) for t in range(m.bit_length())):
            if b:
                piece = flip(piece, b)
        part = out.at[piece, pl.ds(c * UNROLL, UNROLL)]
        return pltpu.make_async_remote_copy(
            src_ref=part, dst_ref=part, send_sem=wss.at[h, c], recv_sem=wrs.at[h, c],
            device_id=(me, flip(mc, bit)), device_id_type=pl.DeviceIdType.MESH)

    firsts = [h for h, (_, m) in enumerate(hops) if m == 0]

    for k in range(FILTER):
        for g in range(groups):
            copy(k, g).wait_recv()
        ys = (y1, y2, y3, None)[k]

        @pl.loop(0, chunks)
        def _(c):
            if k == 0:
                load(c).wait()
            if k in (1, 2):
                for g in range(groups):
                    @pl.when(c == g + 1)
                    def _():
                        pack(k + 1, g, ys, pexp)
            for u in range(UNROLL):
                j = c * UNROLL + u
                value = product(k, j)
                low = value.astype(bf16)
                if k < FILTER - 1:
                    xs[k + 1][j] = low
                    ys[j] = value
                else:
                    out[mc, j] = low
                if k == FILTER - 1 and u == 1:
                    @pl.when(c > 0)
                    def _():
                        for h in firsts:
                            spread(h, c - 1).start()
                if k in (1, 2) and u == 1:
                    for g in range(groups):
                        @pl.when(c == g + 1)
                        def _():
                            copy(k + 1, g).start()

        if k == 0:
            for g in range(groups):
                pack(1, g, ys, pexn)
            for g in range(groups):
                copy(1, g).start()

    for k in range(FILTER):
        for g in range(groups):
            copy(k, g).wait_send()
    for h in firsts:
        spread(h, chunks - 1).start()

    @pl.loop(0, chunks)
    def _(c):
        got = set()
        for h, (bit, m) in enumerate(hops):
            if m:
                source = max(hh for hh in range(h) if hops[hh][0] + hops[hh][1] == m)
                if source not in got:
                    spread(source, c).wait_recv()
                    got.add(source)
                spread(h, c).start()
    relayed = {max(hh for hh in range(h) if hops[hh][0] + hops[hh][1] == m)
               for h, (_, m) in enumerate(hops) if m}

    @pl.loop(0, chunks)
    def _(c):
        for h in range(len(hops)):
            if h not in relayed:
                spread(h, c).wait_recv()
            spread(h, c).wait_send()

    gp[...] = jnp.zeros_like(gp)

    @pl.loop(0, lb // 8)
    def _(c):
        cat = [jnp.concatenate([out[q, c * 8 + u] for u in range(8)], axis=1)
               for q in range(parts)]
        left = jnp.concatenate([out[mc, c * 8 + u] for u in range(8)], axis=1)
        gp[...] += lax.dot_general(left, jnp.concatenate(cat, axis=0), (((1,), (1,)), ((), ())),
                                   preferred_element_type=f32)

    def part_to(d):
        to = lax.rem(me + d, rows)
        lo = pl.multiple_of(to * rps, rps)
        return to, pltpu.make_async_remote_copy(
            src_ref=gp.at[pl.ds(lo, rps)], dst_ref=rb.at[d], send_sem=pss.at[d],
            recv_sem=prs.at[d], device_id=(to, mc), device_id_type=pl.DeviceIdType.MESH)

    def part_in(d):
        return pltpu.make_async_remote_copy(
            src_ref=gp.at[pl.ds(0, rps)], dst_ref=rb.at[d], send_sem=pss.at[d],
            recv_sem=prs.at[d], device_id=(lax.rem(me + 1, rows), mc),
            device_id_type=pl.DeviceIdType.MESH)

    def only(cond, run):
        if reducers == rows:
            run()
        else:
            pl.when(cond)(run)

    @pl.loop(1, rows)
    def _(d):
        to, c = part_to(d)
        only(to < reducers, lambda: c.start())

    def all_to(e, sender):
        to = lax.rem(linear + e, everyone)
        lo = pl.multiple_of((lax.rem(sender, parts) * reducers + sender // parts) * rps, rps)
        return pltpu.make_async_remote_copy(
            src_ref=gs, dst_ref=gram.at[pl.ds(lo, rps)], send_sem=ass.at[e],
            recv_sem=ars.at[e], device_id=(to // parts, lax.rem(to, parts)),
            device_id_type=pl.DeviceIdType.MESH)

    def reduce():
        lo = pl.multiple_of(me * rps, rps)
        total = gp[pl.ds(lo, rps)]
        for d in range(1, rows):
            part_in(d).wait_recv()
            total = total + rb[d]
        gs[...] = total
        gram[pl.ds(pl.multiple_of((mc * reducers + me) * rps, rps), rps)] = total

        @pl.loop(1, everyone)
        def _(e):
            all_to(e, linear).start()

    only(me < reducers, reduce)

    @pl.loop(1, rows)
    def _(d):
        to, c = part_to(d)
        only(to < reducers, lambda: c.wait_send())

    @pl.loop(1, everyone)
    def _(e):
        sender = lax.rem(linear - e + everyone, everyone)
        only(me < reducers, lambda: all_to(e, linear).wait_send())
        only(sender // parts < reducers, lambda: all_to(e, sender).wait_recv())


def filtered(subspace, onsite, blocks, cols):
    rows, parts = lax.axis_size("row"), lax.axis_size("col")
    me = lax.axis_index("row")
    everyone, hops = rows * parts, len(hops_of(parts))
    width = subspace.shape[0]
    sc, lb, bs, _ = blocks.shape
    groups = len(shifts_of(rows))
    tab = index_tables(cols, rows, me, lb)
    ext = lb + groups * HALO
    vm, dma = pltpu.VMEM, pltpu.SemaphoreType.DMA
    full = parts * width
    rps = slice_of(width, rows)
    return pl.pallas_call(
        functools.partial(filter_kernel, rows, parts, lb, sc),
        out_shape=(jax.ShapeDtypeStruct((parts, lb, width, bs), bf16),
                   jax.ShapeDtypeStruct((full, full), f32)),
        in_specs=[pl.BlockSpec(memory_space=pltpu.SMEM), pl.BlockSpec(memory_space=pl.ANY),
                  pl.BlockSpec(memory_space=pltpu.VMEM), pl.BlockSpec(memory_space=pl.ANY)],
        out_specs=[pl.BlockSpec(memory_space=pltpu.VMEM)] * 2,
        scratch_shapes=[vm((sc, lb, bs, bs), bf16)]
        + [vm((ext, width, bs), bf16)] * 4
        + [vm((lb, width, bs), bf16)]
        + [vm((lb, width, bs), f32)] * 3
        + [vm((groups * HALO, width, bs), bf16)] * 4
        + [vm((width, full), f32), vm((rps, full), f32), vm((rows, rps, full), f32)]
        + [dma((lb // UNROLL,)), dma((lb,)), dma((lb,)), dma((FILTER, groups)), dma((FILTER, groups)),
           dma((hops, lb // UNROLL)), dma((hops, lb // UNROLL)), dma((rows,)), dma((rows,)),
           dma((everyone,)), dma((everyone,))],
        compiler_params=pltpu.CompilerParams(
            collective_id=0, has_side_effects=True, vmem_limit_bytes=56 * 1024 * 1024),
        name="filter",
    )(tab, subspace, onsite.reshape(lb, 1, bs), blocks)


def eliminate(src, up, low):
    n = src.shape[0]
    tiles = n // 8
    a = [src[8 * t:8 * t + 8, :] for t in range(tiles)]
    sub = lax.broadcasted_iota(jnp.int32, (8, n), 0)
    lane = lax.broadcasted_iota(jnp.int32, (8, n), 1)
    b = [jnp.where(lane == sub + 8 * t, 1.0, 0.0).astype(f32) for t in range(tiles)]

    def row(v, q):
        return jnp.broadcast_to(v[q:q + 1, :], (8, n))

    for p in range(tiles):
        cols = {t: [jnp.broadcast_to(a[t][:, 8 * p + q:8 * p + q + 1], (8, n)) for q in range(8)]
                for t in range(p, tiles)}
        pivots = jnp.ones((8, n), f32)
        for q in range(8):
            pivot = row(cols[p][q], q)
            pivots = jnp.where(sub == q, pivot, pivots)
            inverse = 1.0 / pivot
            right = [row(cols[p][k], q) for k in range(8)]
            arow, brow = row(a[p], q), row(b[p], q)
            for t in range(p, tiles):
                m = cols[t][q] * inverse
                if t == p:
                    m = jnp.where(sub > q, m, 0.0)
                for k in range(q + 1, 8):
                    cols[t][k] = cols[t][k] - m * right[k]
                a[t] = a[t] - m * arow
                b[t] = b[t] - m * brow
        scale = lax.rsqrt(pivots)
        up[8 * p:8 * p + 8, :] = jnp.where(lane >= sub + 8 * p, a[p] * scale, 0.0)
        low[8 * p:8 * p + 8, :] = b[p] * scale


def finish_kernel(root, col, whole, gram, basis, factor, work, up, low, inv):
    parts, lb, width, bs = whole.shape
    full = gram.shape[0]
    half = full // 2
    exact = functools.partial(lax.dot_general, precision=lax.Precision.HIGHEST,
                              preferred_element_type=f32)
    nn, nt, tn = ((((1,), (0,)), ((), ())), (((1,), (1,)), ((), ())), (((0,), (0,)), ((), ())))
    work[...] = gram[:half, :half]
    factor[half:, :half] = jnp.zeros((half, half), f32)
    inv[:half, half:] = jnp.zeros((half, half), f32)

    @pl.loop(0, 2)
    def _(i):
        eliminate(work, up.at[i], low.at[i])

        @pl.when(i == 0)
        def _():
            across = exact(low[0], gram[:half, half:], nn)
            factor[:half, half:] = across * (1.0 / root)
            work[...] = gram[half:, half:] - exact(across, across, tn)

    across = factor[:half, half:] * root
    inv[:half, :half] = low[0]
    inv[half:, half:] = low[1]
    inv[half:, :half] = -exact(low[1], exact(across, low[0], tn), nn)
    factor[:half, :half] = up[0] * (1.0 / root)
    factor[half:, half:] = up[1] * (1.0 / root)

    mine = inv[pl.ds(pl.multiple_of(col[0] * width, width), width), :] * root
    high = mine.astype(bf16)
    rest = mine - high.astype(f32)
    mid = rest.astype(bf16)
    last = (rest - mid.astype(f32)).astype(bf16)
    left = jnp.concatenate([high, mid, last], axis=0)

    for k in range(lb):
        right = jnp.concatenate([whole[q, k] for q in range(parts)], axis=0)
        r = jnp.dot(left, right, preferred_element_type=f32)
        basis[:, k * bs:(k + 1) * bs] = r[:width] + (r[width:2 * width] + r[2 * width:])


def body(subspace, onsite, blocks, cols):
    row_count = lax.axis_size("row")
    part_width, local_rows = subspace.shape
    whole, gram = filtered(subspace, onsite, blocks, cols)
    full = gram.shape[0]
    half = full // 2
    root = math.sqrt(row_count * local_rows)
    vm = pltpu.VMEM
    return pl.pallas_call(
        functools.partial(finish_kernel, root),
        out_shape=(jax.ShapeDtypeStruct((part_width, local_rows), f32),
                   jax.ShapeDtypeStruct((full, full), f32)),
        in_specs=[pl.BlockSpec(memory_space=pltpu.SMEM)] + [pl.BlockSpec(memory_space=vm)] * 2,
        out_specs=[pl.BlockSpec(memory_space=vm)] * 2,
        scratch_shapes=[vm((half, half), f32), vm((2, half, half), f32), vm((2, half, half), f32),
                        vm((full, full), f32)],
        compiler_params=pltpu.CompilerParams(vmem_limit_bytes=32 * 1024 * 1024),
        name="finish",
    )(lax.axis_index("col").astype(jnp.int32).reshape(1), whole, gram)


def solution(mesh):
    in_specs = (P("col", "row"), P("row"), P(None, "row", None, None), P())
    out_specs = (P("col", "row"), P())
    return jax.shard_map(body, mesh=mesh, in_specs=in_specs, out_specs=out_specs, check_vma=False)
```

```python
import functools
import math

import jax
import jax.numpy as jnp
from jax import lax
from jax.experimental import pallas as pl
from jax.experimental.pallas import tpu as pltpu
from jax.sharding import PartitionSpec as P

HALO = 4
FILTER = 4
UNROLL = 4
HALVES = 2
filter_scale = 0.4
f32 = jnp.float32
bf16 = jnp.bfloat16


def shifts_of(rows):
    return (rows // 2, 2, 1, -1)


def index_tables(cols, rows, me, lb):
    sc = cols.shape[1]
    shifts = shifts_of(rows)
    groups = len(shifts)
    own = lax.dynamic_slice_in_dim(cols, me * lb, lb, 0).reshape(-1)
    askers = [
        lax.dynamic_slice_in_dim(cols, lax.rem(me - d + rows, rows) * lb, lb, 0).reshape(-1)
        for d in shifts
    ]
    owners = jnp.stack([lax.rem(me + d + rows, rows) for d in shifts])
    k = jnp.arange(lb, dtype=jnp.int32)
    wanted = own[None, :] - owners[:, None] * lb
    asked = jnp.stack(askers) - me * lb
    rel = jnp.concatenate([wanted, asked], 0)
    hit = jnp.any(rel[:, :, None] == k, axis=1)
    before = (k[:, None] < k[None, :])
    rank = jnp.sum((hit[:, :, None] & before[None]).astype(jnp.int32), axis=1)
    hit_e, rank_e = hit[groups:], rank[groups:]
    g = jnp.arange(groups, dtype=jnp.int32)
    key = jnp.min(jnp.where(hit_e, g[:, None], groups), axis=0)
    ahead = (key[:, None] < key[None, :]) | ((key[:, None] == key[None, :]) & before)
    inv = jnp.sum(ahead.astype(jnp.int32), axis=0)
    perm = jnp.sum(jnp.where(inv[None, :] == k[:, None], k[None, :], 0), axis=1)
    m = jnp.arange(HALO, dtype=jnp.int32)
    pick = hit_e[:, None, :] & (rank_e[:, None, :] == m[:, None])
    exp_n = jnp.sum(jnp.where(pick, k, 0), axis=-1)
    exp_p = jnp.sum(jnp.where(pick, inv, 0), axis=-1)
    slot = lb + HALO * g[:, None] + rank[:groups]
    match = wanted[:, :, None] == k
    far = jnp.sum(jnp.where(match, slot[:, None, :], 0), axis=(0, 2))
    near = own - me * lb
    mine = (near >= 0) & (near < lb)
    near_p = jnp.sum(jnp.where(near[:, None] == k, inv, 0), axis=1)
    pos_n = jnp.where(mine, near, far)
    pos_p = jnp.where(mine, near_p, far)
    return jnp.concatenate(
        [pos_n, pos_p, perm, inv, exp_n.reshape(-1), exp_p.reshape(-1)]
    ).astype(jnp.int32)


def flip(c, bit):
    return c + bit - 2 * bit * lax.rem(c // bit, 2)


def hops_of(parts):
    hops, held, bit = [], [0], parts // 2
    while bit:
        hops += [(bit, m) for m in held]
        held += [m + bit for m in held]
        bit //= 2
    return hops


def slice_of(width, rows):
    return max(8, width // rows)


def filter_kernel(rows, parts, lb, sc, tab, sub, ons, blk, out, gram, bm, *refs):
    refs = list(refs)
    take = lambda n: [refs.pop(0) for _ in range(n)]
    halves = range(HALVES)
    xs = [take(HALVES) for _ in range(FILTER)]
    snds = [take(HALVES) for _ in range(FILTER)]
    ys = [take(HALVES) for _ in range(FILTER - 1)]
    s0 = take(HALVES)
    gp, gs, rb, bsem, xsem, csem, ssem, rsem, wss, wrs, pss, prs, ass, ars = refs
    me = lax.axis_index("row")
    mc = lax.axis_index("col")
    everyone = rows * parts
    linear = me * parts + mc
    hw = out.shape[2]
    width = hw * HALVES
    hops = hops_of(parts)
    rps = slice_of(width, rows)
    reducers = width // rps
    shifts = shifts_of(rows)
    groups = len(shifts)
    pn, pp = 0, lb * sc
    pperm = 2 * lb * sc
    pinv = pperm + lb
    pexn = pinv + lb
    pexp = pexn + groups * HALO
    bs = blk.shape[-1]
    chunks = lb // UNROLL

    def load(c):
        part = pl.ds(c * UNROLL, UNROLL)
        return pltpu.make_async_copy(blk.at[:, part], bm.at[:, part], bsem.at[c])

    def first(i, h):
        cut = sub.at[pl.ds(h * hw, hw), pl.ds(pl.multiple_of(i * bs, bs), bs)]
        return (pltpu.make_async_copy(cut, xs[0][h].at[i], xsem.at[h, i]),
                pltpu.make_async_copy(cut, s0[h].at[i], csem.at[h, i]))

    for h in halves:
        @pl.loop(0, lb)
        def _(i):
            a, b = first(i, h)
            b.start()
            a.start()

    @pl.loop(0, chunks)
    def _(c):
        load(c).start()

    barrier = pltpu.get_barrier_semaphore()

    @pl.loop(1, everyone)
    def _(e):
        to = lax.rem(linear + e, everyone)
        pl.semaphore_signal(barrier, inc=1, device_id=(to // parts, lax.rem(to, parts)),
                            device_id_type=pl.DeviceIdType.MESH)

    def copy(k, h, g):
        return pltpu.make_async_remote_copy(
            src_ref=snds[k][h].at[pl.ds(g * HALO, HALO)],
            dst_ref=xs[k][h].at[pl.ds(lb + g * HALO, HALO)],
            send_sem=ssem.at[k, h, g], recv_sem=rsem.at[k, h, g],
            device_id=(lax.rem(me - shifts[g] + rows, rows), mc),
            device_id_type=pl.DeviceIdType.MESH)

    def pack(k, h, g, source, base):
        for m in range(HALO):
            snds[k][h][g * HALO + m] = source[tab[base + g * HALO + m]].astype(bf16)

    for h in halves:
        @pl.loop(0, lb)
        def _(i):
            first(i, h)[1].wait()

        for g in range(groups):
            pack(0, h, g, s0[h], pexn)
        if h == 0:
            pl.semaphore_wait(barrier, everyone - 1)
        for g in range(groups):
            copy(0, h, g).start()

    for h in halves:
        @pl.loop(0, lb)
        def _(i):
            first(i, h)[0].wait()

    def product(k, h, j):
        i = j if k == FILTER - 1 else tab[pperm + j]
        own = tab[pinv + j] if k == FILTER - 1 else (i if k == 0 else j)
        base = pn if k == 0 else pp
        x = xs[k][h]
        left = jnp.concatenate([x[tab[base + i * sc + s]] for s in range(sc)], axis=1)
        right = jnp.concatenate([bm[s, i] for s in range(sc)], axis=0)
        acc = jnp.dot(left, right, preferred_element_type=f32)
        total = acc + ons[i] * x[own].astype(f32)
        if k == 0:
            return filter_scale * total
        prev = xs[0][h][i].astype(f32) if k == 1 else ys[k - 2][h][own]
        return 2.0 * filter_scale * total - prev

    def spread(n, h, c):
        bit, m = hops[n]
        piece = mc
        for b in (m & (1 << t) for t in range(m.bit_length())):
            if b:
                piece = flip(piece, b)
        part = out.at[piece * HALVES + h, pl.ds(c * UNROLL, UNROLL)]
        return pltpu.make_async_remote_copy(
            src_ref=part, dst_ref=part, send_sem=wss.at[n, h, c], recv_sem=wrs.at[n, h, c],
            device_id=(me, flip(mc, bit)), device_id_type=pl.DeviceIdType.MESH)

    firsts = [n for n, (_, m) in enumerate(hops) if m == 0]

    @pl.loop(0, chunks)
    def _(c):
        load(c).wait()

    for k in range(FILTER):
        for h in halves:
            for g in range(groups):
                copy(k, h, g).wait_recv()

            @pl.loop(0, chunks)
            def _(c):
                if k < FILTER - 1:
                    for g in range(groups):
                        @pl.when(c == g + 1)
                        def _():
                            pack(k + 1, h, g, ys[k][h], pexp)
                for u in range(UNROLL):
                    j = c * UNROLL + u
                    value = product(k, h, j)
                    low = value.astype(bf16)
                    if k < FILTER - 1:
                        xs[k + 1][h][j] = low
                        ys[k][h][j] = value
                        if u == 1:
                            for g in range(groups):
                                @pl.when(c == g + 1)
                                def _():
                                    copy(k + 1, h, g).start()
                    else:
                        out[mc * HALVES + h, j] = low
                        if u == 1:
                            @pl.when(c > 0)
                            def _():
                                for n in firsts:
                                    spread(n, h, c - 1).start()
            if k == FILTER - 1:
                for n in firsts:
                    spread(n, h, chunks - 1).start()

    for k in range(FILTER):
        for h in halves:
            for g in range(groups):
                copy(k, h, g).wait_send()

    needs = {n: max(q for q in range(n) if sum(hops[q]) == m)
             for n, (_, m) in enumerate(hops) if m}
    for h in halves:
        @pl.loop(0, chunks)
        def _(c):
            got = set()
            for n in needs:
                if needs[n] not in got:
                    spread(needs[n], h, c).wait_recv()
                    got.add(needs[n])
                spread(n, h, c).start()
    for h in halves:
        @pl.loop(0, chunks)
        def _(c):
            for n in range(len(hops)):
                if n not in needs.values():
                    spread(n, h, c).wait_recv()
                spread(n, h, c).wait_send()

    gp[...] = jnp.zeros_like(gp)

    @pl.loop(0, lb // 8)
    def _(c):
        cat = [jnp.concatenate([out[q, c * 8 + u] for u in range(8)], axis=1)
               for q in range(parts * HALVES)]
        left = jnp.concatenate([jnp.concatenate([out[mc * HALVES + h, c * 8 + u]
                                                 for u in range(8)], axis=1)
                                for h in halves], axis=0)
        gp[...] += lax.dot_general(left, jnp.concatenate(cat, axis=0), (((1,), (1,)), ((), ())),
                                   preferred_element_type=f32)

    def part_to(d):
        to = lax.rem(me + d, rows)
        lo = pl.multiple_of(to * rps, rps)
        return to, pltpu.make_async_remote_copy(
            src_ref=gp.at[pl.ds(lo, rps)], dst_ref=rb.at[d], send_sem=pss.at[d],
            recv_sem=prs.at[d], device_id=(to, mc), device_id_type=pl.DeviceIdType.MESH)

    def part_in(d):
        return pltpu.make_async_remote_copy(
            src_ref=gp.at[pl.ds(0, rps)], dst_ref=rb.at[d], send_sem=pss.at[d],
            recv_sem=prs.at[d], device_id=(lax.rem(me + 1, rows), mc),
            device_id_type=pl.DeviceIdType.MESH)

    def only(cond, run):
        if reducers == rows:
            run()
        else:
            pl.when(cond)(run)

    @pl.loop(1, rows)
    def _(d):
        to, c = part_to(d)
        only(to < reducers, lambda: c.start())

    def all_to(e, sender):
        to = lax.rem(linear + e, everyone)
        lo = pl.multiple_of((lax.rem(sender, parts) * reducers + sender // parts) * rps, rps)
        return pltpu.make_async_remote_copy(
            src_ref=gs, dst_ref=gram.at[pl.ds(lo, rps)], send_sem=ass.at[e],
            recv_sem=ars.at[e], device_id=(to // parts, lax.rem(to, parts)),
            device_id_type=pl.DeviceIdType.MESH)

    def reduce():
        lo = pl.multiple_of(me * rps, rps)
        total = gp[pl.ds(lo, rps)]
        for d in range(1, rows):
            part_in(d).wait_recv()
            total = total + rb[d]
        gs[...] = total
        gram[pl.ds(pl.multiple_of((mc * reducers + me) * rps, rps), rps)] = total

        @pl.loop(1, everyone)
        def _(e):
            all_to(e, linear).start()

    only(me < reducers, reduce)

    @pl.loop(1, rows)
    def _(d):
        to, c = part_to(d)
        only(to < reducers, lambda: c.wait_send())

    @pl.loop(1, everyone)
    def _(e):
        sender = lax.rem(linear - e + everyone, everyone)
        only(me < reducers, lambda: all_to(e, linear).wait_send())
        only(sender // parts < reducers, lambda: all_to(e, sender).wait_recv())


def filtered(subspace, onsite, blocks, cols):
    rows, parts = lax.axis_size("row"), lax.axis_size("col")
    me = lax.axis_index("row")
    everyone, hops = rows * parts, len(hops_of(parts))
    width = subspace.shape[0]
    sc, lb, bs, _ = blocks.shape
    groups = len(shifts_of(rows))
    tab = index_tables(cols, rows, me, lb)
    ext = lb + groups * HALO
    vm, dma = pltpu.VMEM, pltpu.SemaphoreType.DMA
    full, hw = parts * width, width // HALVES
    rps = slice_of(width, rows)
    return pl.pallas_call(
        functools.partial(filter_kernel, rows, parts, lb, sc),
        out_shape=(jax.ShapeDtypeStruct((parts * HALVES, lb, hw, bs), bf16),
                   jax.ShapeDtypeStruct((full, full), f32)),
        in_specs=[pl.BlockSpec(memory_space=pltpu.SMEM), pl.BlockSpec(memory_space=pl.ANY),
                  pl.BlockSpec(memory_space=pltpu.VMEM), pl.BlockSpec(memory_space=pl.ANY)],
        out_specs=[pl.BlockSpec(memory_space=pltpu.VMEM)] * 2,
        scratch_shapes=[vm((sc, lb, bs, bs), bf16)]
        + [vm((ext, hw, bs), bf16)] * (FILTER * HALVES)
        + [vm((groups * HALO, hw, bs), bf16)] * (FILTER * HALVES)
        + [vm((lb, hw, bs), f32)] * ((FILTER - 1) * HALVES)
        + [vm((lb, hw, bs), bf16)] * HALVES
        + [vm((width, full), f32), vm((rps, full), f32), vm((rows, rps, full), f32)]
        + [dma((lb // UNROLL,)), dma((HALVES, lb)), dma((HALVES, lb)),
           dma((FILTER, HALVES, groups)), dma((FILTER, HALVES, groups)),
           dma((hops, HALVES, lb // UNROLL)), dma((hops, HALVES, lb // UNROLL)),
           dma((rows,)), dma((rows,)), dma((everyone,)), dma((everyone,))],
        compiler_params=pltpu.CompilerParams(
            collective_id=0, has_side_effects=True, vmem_limit_bytes=56 * 1024 * 1024),
        name="filter",
    )(tab, subspace, onsite.reshape(lb, 1, bs), blocks)


def eliminate(src, up, low):
    n = src.shape[0]
    tiles = n // 8
    a = [src[8 * t:8 * t + 8, :] for t in range(tiles)]
    sub = lax.broadcasted_iota(jnp.int32, (8, n), 0)
    lane = lax.broadcasted_iota(jnp.int32, (8, n), 1)
    b = [jnp.where(lane == sub + 8 * t, 1.0, 0.0).astype(f32) for t in range(tiles)]

    def row(v, q):
        return jnp.broadcast_to(v[q:q + 1, :], (8, n))

    for p in range(tiles):
        cols = {t: [jnp.broadcast_to(a[t][:, 8 * p + q:8 * p + q + 1], (8, n)) for q in range(8)]
                for t in range(p, tiles)}
        pivots = jnp.ones((8, n), f32)
        for q in range(8):
            pivot = row(cols[p][q], q)
            pivots = jnp.where(sub == q, pivot, pivots)
            inverse = 1.0 / pivot
            right = [row(cols[p][k], q) for k in range(8)]
            arow, brow = row(a[p], q), row(b[p], q)
            for t in range(p, tiles):
                m = cols[t][q] * inverse
                if t == p:
                    m = jnp.where(sub > q, m, 0.0)
                for k in range(q + 1, 8):
                    cols[t][k] = cols[t][k] - m * right[k]
                a[t] = a[t] - m * arow
                b[t] = b[t] - m * brow
        scale = lax.rsqrt(pivots)
        up[8 * p:8 * p + 8, :] = jnp.where(lane >= sub + 8 * p, a[p] * scale, 0.0)
        low[8 * p:8 * p + 8, :] = b[p] * scale


def finish_kernel(root, col, whole, gram, basis, factor, work, up, low, inv):
    parts, lb, _, bs = whole.shape
    width = basis.shape[0]
    full = gram.shape[0]
    half = full // 2
    exact = functools.partial(lax.dot_general, precision=lax.Precision.HIGHEST,
                              preferred_element_type=f32)
    nn, nt, tn = ((((1,), (0,)), ((), ())), (((1,), (1,)), ((), ())), (((0,), (0,)), ((), ())))
    work[...] = gram[:half, :half]
    factor[half:, :half] = jnp.zeros((half, half), f32)
    inv[:half, half:] = jnp.zeros((half, half), f32)

    @pl.loop(0, 2)
    def _(i):
        eliminate(work, up.at[i], low.at[i])

        @pl.when(i == 0)
        def _():
            across = exact(low[0], gram[:half, half:], nn)
            factor[:half, half:] = across * (1.0 / root)
            work[...] = gram[half:, half:] - exact(across, across, tn)

    across = factor[:half, half:] * root
    inv[:half, :half] = low[0]
    inv[half:, half:] = low[1]
    inv[half:, :half] = -exact(low[1], exact(across, low[0], tn), nn)
    factor[:half, :half] = up[0] * (1.0 / root)
    factor[half:, half:] = up[1] * (1.0 / root)

    mine = inv[pl.ds(pl.multiple_of(col[0] * width, width), width), :] * root
    high = mine.astype(bf16)
    rest = mine - high.astype(f32)
    mid = rest.astype(bf16)
    last = (rest - mid.astype(f32)).astype(bf16)
    left = jnp.concatenate([high, mid, last], axis=0)

    for k in range(lb):
        right = jnp.concatenate([whole[q, k] for q in range(parts)], axis=0)
        r = jnp.dot(left, right, preferred_element_type=f32)
        basis[:, k * bs:(k + 1) * bs] = r[:width] + (r[width:2 * width] + r[2 * width:])


def body(subspace, onsite, blocks, cols):
    row_count = lax.axis_size("row")
    part_width, local_rows = subspace.shape
    whole, gram = filtered(subspace, onsite, blocks, cols)
    full = gram.shape[0]
    half = full // 2
    root = math.sqrt(row_count * local_rows)
    vm = pltpu.VMEM
    return pl.pallas_call(
        functools.partial(finish_kernel, root),
        out_shape=(jax.ShapeDtypeStruct((part_width, local_rows), f32),
                   jax.ShapeDtypeStruct((full, full), f32)),
        in_specs=[pl.BlockSpec(memory_space=pltpu.SMEM)] + [pl.BlockSpec(memory_space=vm)] * 2,
        out_specs=[pl.BlockSpec(memory_space=vm)] * 2,
        scratch_shapes=[vm((half, half), f32), vm((2, half, half), f32), vm((2, half, half), f32),
                        vm((full, full), f32)],
        compiler_params=pltpu.CompilerParams(vmem_limit_bytes=32 * 1024 * 1024),
        name="finish",
    )(lax.axis_index("col").astype(jnp.int32).reshape(1), whole, gram)


def solution(mesh):
    in_specs = (P("col", "row"), P("row"), P(None, "row", None, None), P())
    out_specs = (P("col", "row"), P())
    return jax.shard_map(body, mesh=mesh, in_specs=in_specs, out_specs=out_specs, check_vma=False)
```

```python
import functools
import math

import jax
import jax.numpy as jnp
from jax import lax
from jax.experimental import pallas as pl
from jax.experimental.pallas import tpu as pltpu
from jax.sharding import PartitionSpec as P

HALO = 4
FILTER = 4
UNROLL = 4
HALVES = 1
filter_scale = 0.4
f32 = jnp.float32
bf16 = jnp.bfloat16


def shifts_of(rows):
    return (rows // 2, 2, 1, -1)


def index_tables(cols, rows, me, lb):
    sc = cols.shape[1]
    shifts = shifts_of(rows)
    groups = len(shifts)
    own = lax.dynamic_slice_in_dim(cols, me * lb, lb, 0).reshape(-1)
    askers = [
        lax.dynamic_slice_in_dim(cols, lax.rem(me - d + rows, rows) * lb, lb, 0).reshape(-1)
        for d in shifts
    ]
    owners = jnp.stack([lax.rem(me + d + rows, rows) for d in shifts])
    k = jnp.arange(lb, dtype=jnp.int32)
    wanted = own[None, :] - owners[:, None] * lb
    asked = jnp.stack(askers) - me * lb
    rel = jnp.concatenate([wanted, asked], 0)
    hit = jnp.any(rel[:, :, None] == k, axis=1)
    before = (k[:, None] < k[None, :])
    rank = jnp.sum((hit[:, :, None] & before[None]).astype(jnp.int32), axis=1)
    hit_e, rank_e = hit[groups:], rank[groups:]
    g = jnp.arange(groups, dtype=jnp.int32)
    key = jnp.min(jnp.where(hit_e, g[:, None], groups), axis=0)
    ahead = (key[:, None] < key[None, :]) | ((key[:, None] == key[None, :]) & before)
    inv = jnp.sum(ahead.astype(jnp.int32), axis=0)
    perm = jnp.sum(jnp.where(inv[None, :] == k[:, None], k[None, :], 0), axis=1)
    m = jnp.arange(HALO, dtype=jnp.int32)
    pick = hit_e[:, None, :] & (rank_e[:, None, :] == m[:, None])
    exp_n = jnp.sum(jnp.where(pick, k, 0), axis=-1)
    exp_p = jnp.sum(jnp.where(pick, inv, 0), axis=-1)
    slot = lb + HALO * g[:, None] + rank[:groups]
    match = wanted[:, :, None] == k
    far = jnp.sum(jnp.where(match, slot[:, None, :], 0), axis=(0, 2))
    near = own - me * lb
    mine = (near >= 0) & (near < lb)
    near_p = jnp.sum(jnp.where(near[:, None] == k, inv, 0), axis=1)
    pos_n = jnp.where(mine, near, far)
    pos_p = jnp.where(mine, near_p, far)
    return jnp.concatenate(
        [pos_n, pos_p, perm, inv, exp_n.reshape(-1), exp_p.reshape(-1)]
    ).astype(jnp.int32)


def flip(c, bit):
    return c + bit - 2 * bit * lax.rem(c // bit, 2)


def hops_of(parts):
    hops, held, bit = [], [0], parts // 2
    while bit:
        hops += [(bit, m) for m in held]
        held += [m + bit for m in held]
        bit //= 2
    return hops


def slice_of(width, rows):
    return max(8, width // rows)


def filter_kernel(rows, parts, lb, sc, tab, sub, ons, blk, out, gram, bm, *refs):
    refs = list(refs)
    take = lambda n: [refs.pop(0) for _ in range(n)]
    halves = range(HALVES)
    xs = [take(HALVES) for _ in range(FILTER)]
    snds = [take(HALVES) for _ in range(FILTER)]
    ys = [take(HALVES) for _ in range(FILTER - 1)]
    s0 = take(HALVES)
    gp, gs, rb, bsem, xsem, csem, ssem, rsem, wss, wrs, pss, prs, ass, ars = refs
    me = lax.axis_index("row")
    mc = lax.axis_index("col")
    everyone = rows * parts
    linear = me * parts + mc
    hw = out.shape[2]
    width = hw * HALVES
    hops = hops_of(parts)
    rps = slice_of(width, rows)
    reducers = width // rps
    shifts = shifts_of(rows)
    groups = len(shifts)
    pn, pp = 0, lb * sc
    pperm = 2 * lb * sc
    pinv = pperm + lb
    pexn = pinv + lb
    pexp = pexn + groups * HALO
    bs = blk.shape[-1]
    chunks = lb // UNROLL

    def load(c):
        part = pl.ds(c * UNROLL, UNROLL)
        return pltpu.make_async_copy(blk.at[:, part], bm.at[:, part], bsem.at[c])

    def first(i, h):
        cut = sub.at[pl.ds(h * hw, hw), pl.ds(pl.multiple_of(i * bs, bs), bs)]
        return (pltpu.make_async_copy(cut, xs[0][h].at[i], xsem.at[h, i]),
                pltpu.make_async_copy(cut, s0[h].at[i], csem.at[h, i]))

    for h in halves:
        @pl.loop(0, lb)
        def _(i):
            a, b = first(i, h)
            b.start()
            a.start()

    @pl.loop(0, chunks)
    def _(c):
        load(c).start()

    barrier = pltpu.get_barrier_semaphore()

    @pl.loop(1, everyone)
    def _(e):
        to = lax.rem(linear + e, everyone)
        pl.semaphore_signal(barrier, inc=1, device_id=(to // parts, lax.rem(to, parts)),
                            device_id_type=pl.DeviceIdType.MESH)

    def copy(k, h, g):
        return pltpu.make_async_remote_copy(
            src_ref=snds[k][h].at[pl.ds(g * HALO, HALO)],
            dst_ref=xs[k][h].at[pl.ds(lb + g * HALO, HALO)],
            send_sem=ssem.at[k, h, g], recv_sem=rsem.at[k, h, g],
            device_id=(lax.rem(me - shifts[g] + rows, rows), mc),
            device_id_type=pl.DeviceIdType.MESH)

    def pack(k, h, g, source, base):
        for m in range(HALO):
            snds[k][h][g * HALO + m] = source[tab[base + g * HALO + m]].astype(bf16)

    for h in halves:
        @pl.loop(0, lb)
        def _(i):
            first(i, h)[1].wait()

        for g in range(groups):
            pack(0, h, g, s0[h], pexn)
        if h == 0:
            pl.semaphore_wait(barrier, everyone - 1)
        for g in range(groups):
            copy(0, h, g).start()

    for h in halves:
        @pl.loop(0, lb)
        def _(i):
            first(i, h)[0].wait()

    def product(k, h, j):
        i = j if k == FILTER - 1 else tab[pperm + j]
        own = tab[pinv + j] if k == FILTER - 1 else (i if k == 0 else j)
        base = pn if k == 0 else pp
        x = xs[k][h]
        left = jnp.concatenate([x[tab[base + i * sc + s]] for s in range(sc)], axis=1)
        right = jnp.concatenate([bm[s, i] for s in range(sc)], axis=0)
        acc = jnp.dot(left, right, preferred_element_type=f32)
        total = acc + ons[i] * x[own].astype(f32)
        if k == 0:
            return filter_scale * total
        prev = xs[0][h][i].astype(f32) if k == 1 else ys[k - 2][h][own]
        return 2.0 * filter_scale * total - prev

    def spread(n, h, c):
        bit, m = hops[n]
        piece = mc
        for b in (m & (1 << t) for t in range(m.bit_length())):
            if b:
                piece = flip(piece, b)
        part = out.at[piece * HALVES + h, pl.ds(c * UNROLL, UNROLL)]
        return pltpu.make_async_remote_copy(
            src_ref=part, dst_ref=part, send_sem=wss.at[n, h, c], recv_sem=wrs.at[n, h, c],
            device_id=(me, flip(mc, bit)), device_id_type=pl.DeviceIdType.MESH)

    firsts = [n for n, (_, m) in enumerate(hops) if m == 0]

    @pl.loop(0, chunks)
    def _(c):
        load(c).wait()

    for k in range(FILTER):
        for h in halves:
            for g in range(groups):
                copy(k, h, g).wait_recv()

            @pl.loop(0, chunks)
            def _(c):
                if k < FILTER - 1:
                    for g in range(groups):
                        @pl.when(c == g + 1)
                        def _():
                            pack(k + 1, h, g, ys[k][h], pexp)
                for u in range(UNROLL):
                    j = c * UNROLL + u
                    value = product(k, h, j)
                    low = value.astype(bf16)
                    if k < FILTER - 1:
                        xs[k + 1][h][j] = low
                        ys[k][h][j] = value
                        if u == 1:
                            for g in range(groups):
                                @pl.when(c == g + 1)
                                def _():
                                    copy(k + 1, h, g).start()
                    else:
                        out[mc * HALVES + h, j] = low
                        if u == 1:
                            @pl.when(c > 0)
                            def _():
                                for n in firsts:
                                    spread(n, h, c - 1).start()
            if k == FILTER - 1:
                for n in firsts:
                    spread(n, h, chunks - 1).start()

    for k in range(FILTER):
        for h in halves:
            for g in range(groups):
                copy(k, h, g).wait_send()

    needs = {n: max(q for q in range(n) if sum(hops[q]) == m)
             for n, (_, m) in enumerate(hops) if m}
    for h in halves:
        @pl.loop(0, chunks)
        def _(c):
            got = set()
            for n in needs:
                if needs[n] not in got:
                    spread(needs[n], h, c).wait_recv()
                    got.add(needs[n])
                spread(n, h, c).start()
    for h in halves:
        @pl.loop(0, chunks)
        def _(c):
            for n in range(len(hops)):
                if n not in needs.values():
                    spread(n, h, c).wait_recv()
                spread(n, h, c).wait_send()

    gp[...] = jnp.zeros_like(gp)

    @pl.loop(0, lb // 8)
    def _(c):
        cat = [jnp.concatenate([out[q, c * 8 + u] for u in range(8)], axis=1)
               for q in range(parts * HALVES)]
        left = jnp.concatenate([jnp.concatenate([out[mc * HALVES + h, c * 8 + u]
                                                 for u in range(8)], axis=1)
                                for h in halves], axis=0)
        gp[...] += lax.dot_general(left, jnp.concatenate(cat, axis=0), (((1,), (1,)), ((), ())),
                                   preferred_element_type=f32)

    def part_to(d):
        to = lax.rem(me + d, rows)
        lo = pl.multiple_of(to * rps, rps)
        return to, pltpu.make_async_remote_copy(
            src_ref=gp.at[pl.ds(lo, rps)], dst_ref=rb.at[d], send_sem=pss.at[d],
            recv_sem=prs.at[d], device_id=(to, mc), device_id_type=pl.DeviceIdType.MESH)

    def part_in(d):
        return pltpu.make_async_remote_copy(
            src_ref=gp.at[pl.ds(0, rps)], dst_ref=rb.at[d], send_sem=pss.at[d],
            recv_sem=prs.at[d], device_id=(lax.rem(me + 1, rows), mc),
            device_id_type=pl.DeviceIdType.MESH)

    def only(cond, run):
        if reducers == rows:
            run()
        else:
            pl.when(cond)(run)

    @pl.loop(1, rows)
    def _(d):
        to, c = part_to(d)
        only(to < reducers, lambda: c.start())

    def all_to(e, sender):
        to = lax.rem(linear + e, everyone)
        lo = pl.multiple_of((lax.rem(sender, parts) * reducers + sender // parts) * rps, rps)
        return pltpu.make_async_remote_copy(
            src_ref=gs, dst_ref=gram.at[pl.ds(lo, rps)], send_sem=ass.at[e],
            recv_sem=ars.at[e], device_id=(to // parts, lax.rem(to, parts)),
            device_id_type=pl.DeviceIdType.MESH)

    def reduce():
        lo = pl.multiple_of(me * rps, rps)
        total = gp[pl.ds(lo, rps)]
        for d in range(1, rows):
            part_in(d).wait_recv()
            total = total + rb[d]
        gs[...] = total
        gram[pl.ds(pl.multiple_of((mc * reducers + me) * rps, rps), rps)] = total

        @pl.loop(1, everyone)
        def _(e):
            all_to(e, linear).start()

    only(me < reducers, reduce)

    @pl.loop(1, rows)
    def _(d):
        to, c = part_to(d)
        only(to < reducers, lambda: c.wait_send())

    @pl.loop(1, everyone)
    def _(e):
        sender = lax.rem(linear - e + everyone, everyone)
        only(me < reducers, lambda: all_to(e, linear).wait_send())
        only(sender // parts < reducers, lambda: all_to(e, sender).wait_recv())


def filtered(subspace, onsite, blocks, cols):
    rows, parts = lax.axis_size("row"), lax.axis_size("col")
    me = lax.axis_index("row")
    everyone, hops = rows * parts, len(hops_of(parts))
    width = subspace.shape[0]
    sc, lb, bs, _ = blocks.shape
    groups = len(shifts_of(rows))
    tab = index_tables(cols, rows, me, lb)
    ext = lb + groups * HALO
    vm, dma = pltpu.VMEM, pltpu.SemaphoreType.DMA
    full, hw = parts * width, width // HALVES
    rps = slice_of(width, rows)
    return pl.pallas_call(
        functools.partial(filter_kernel, rows, parts, lb, sc),
        out_shape=(jax.ShapeDtypeStruct((parts * HALVES, lb, hw, bs), bf16),
                   jax.ShapeDtypeStruct((full, full), f32)),
        in_specs=[pl.BlockSpec(memory_space=pltpu.SMEM), pl.BlockSpec(memory_space=pl.ANY),
                  pl.BlockSpec(memory_space=pltpu.VMEM), pl.BlockSpec(memory_space=pl.ANY)],
        out_specs=[pl.BlockSpec(memory_space=pltpu.VMEM)] * 2,
        scratch_shapes=[vm((sc, lb, bs, bs), bf16)]
        + [vm((ext, hw, bs), bf16)] * (FILTER * HALVES)
        + [vm((groups * HALO, hw, bs), bf16)] * (FILTER * HALVES)
        + [vm((lb, hw, bs), f32)] * ((FILTER - 1) * HALVES)
        + [vm((lb, hw, bs), bf16)] * HALVES
        + [vm((width, full), f32), vm((rps, full), f32), vm((rows, rps, full), f32)]
        + [dma((lb // UNROLL,)), dma((HALVES, lb)), dma((HALVES, lb)),
           dma((FILTER, HALVES, groups)), dma((FILTER, HALVES, groups)),
           dma((hops, HALVES, lb // UNROLL)), dma((hops, HALVES, lb // UNROLL)),
           dma((rows,)), dma((rows,)), dma((everyone,)), dma((everyone,))],
        compiler_params=pltpu.CompilerParams(
            collective_id=0, has_side_effects=True, vmem_limit_bytes=56 * 1024 * 1024),
        name="filter",
    )(tab, subspace, onsite.reshape(lb, 1, bs), blocks)


def eliminate(src, up, low):
    n = src.shape[0]
    tiles = n // 8
    a = [src[8 * t:8 * t + 8, :] for t in range(tiles)]
    sub = lax.broadcasted_iota(jnp.int32, (8, n), 0)
    lane = lax.broadcasted_iota(jnp.int32, (8, n), 1)
    b = [jnp.where(lane == sub + 8 * t, 1.0, 0.0).astype(f32) for t in range(tiles)]

    def row(v, q):
        return jnp.broadcast_to(v[q:q + 1, :], (8, n))

    for p in range(tiles):
        cols = {t: [jnp.broadcast_to(a[t][:, 8 * p + q:8 * p + q + 1], (8, n)) for q in range(8)]
                for t in range(p, tiles)}
        pivots = jnp.ones((8, n), f32)
        for q in range(8):
            pivot = row(cols[p][q], q)
            pivots = jnp.where(sub == q, pivot, pivots)
            inverse = 1.0 / pivot
            right = [row(cols[p][k], q) for k in range(8)]
            arow, brow = row(a[p], q), row(b[p], q)
            for t in range(p, tiles):
                m = cols[t][q] * inverse
                if t == p:
                    m = jnp.where(sub > q, m, 0.0)
                for k in range(q + 1, 8):
                    cols[t][k] = cols[t][k] - m * right[k]
                a[t] = a[t] - m * arow
                b[t] = b[t] - m * brow
        scale = lax.rsqrt(pivots)
        up[8 * p:8 * p + 8, :] = jnp.where(lane >= sub + 8 * p, a[p] * scale, 0.0)
        low[8 * p:8 * p + 8, :] = b[p] * scale


def finish_kernel(root, col, stored, gram, basis, factor, work, up, low, inv, whole, sem):
    fetch = pltpu.make_async_copy(stored, whole, sem)
    fetch.start()
    parts, lb, _, bs = whole.shape
    width = basis.shape[0]
    full = gram.shape[0]
    half = full // 2
    exact = functools.partial(lax.dot_general, precision=lax.Precision.HIGHEST,
                              preferred_element_type=f32)
    nn, nt, tn = ((((1,), (0,)), ((), ())), (((1,), (1,)), ((), ())), (((0,), (0,)), ((), ())))
    work[...] = gram[:half, :half]
    factor[half:, :half] = jnp.zeros((half, half), f32)
    inv[:half, half:] = jnp.zeros((half, half), f32)

    @pl.loop(0, 2)
    def _(i):
        eliminate(work, up.at[i], low.at[i])

        @pl.when(i == 0)
        def _():
            across = exact(low[0], gram[:half, half:], nn)
            factor[:half, half:] = across * (1.0 / root)
            work[...] = gram[half:, half:] - exact(across, across, tn)

    across = factor[:half, half:] * root
    inv[:half, :half] = low[0]
    inv[half:, half:] = low[1]
    inv[half:, :half] = -exact(low[1], exact(across, low[0], tn), nn)
    factor[:half, :half] = up[0] * (1.0 / root)
    factor[half:, half:] = up[1] * (1.0 / root)

    mine = inv[pl.ds(pl.multiple_of(col[0] * width, width), width), :] * root
    high = mine.astype(bf16)
    rest = mine - high.astype(f32)
    mid = rest.astype(bf16)
    last = (rest - mid.astype(f32)).astype(bf16)
    left = jnp.concatenate([high, mid, last], axis=0)

    fetch.wait()
    for k in range(lb):
        right = jnp.concatenate([whole[q, k] for q in range(parts)], axis=0)
        r = jnp.dot(left, right, preferred_element_type=f32)
        basis[:, k * bs:(k + 1) * bs] = r[:width] + (r[width:2 * width] + r[2 * width:])


def body(subspace, onsite, blocks, cols):
    row_count = lax.axis_size("row")
    part_width, local_rows = subspace.shape
    whole, gram = filtered(subspace, onsite, blocks, cols)
    full = gram.shape[0]
    half = full // 2
    root = math.sqrt(row_count * local_rows)
    vm = pltpu.VMEM
    return pl.pallas_call(
        functools.partial(finish_kernel, root),
        out_shape=(jax.ShapeDtypeStruct((part_width, local_rows), f32),
                   jax.ShapeDtypeStruct((full, full), f32)),
        in_specs=[pl.BlockSpec(memory_space=pltpu.SMEM), pl.BlockSpec(memory_space=pltpu.HBM),
                  pl.BlockSpec(memory_space=vm)],
        out_specs=[pl.BlockSpec(memory_space=vm)] * 2,
        scratch_shapes=[vm((half, half), f32), vm((2, half, half), f32), vm((2, half, half), f32),
                        vm((full, full), f32), vm(whole.shape, bf16), pltpu.SemaphoreType.DMA],
        compiler_params=pltpu.CompilerParams(vmem_limit_bytes=32 * 1024 * 1024),
        name="finish",
    )(lax.axis_index("col").astype(jnp.int32).reshape(1), whole, gram)


def solution(mesh):
    in_specs = (P("col", "row"), P("row"), P(None, "row", None, None), P())
    out_specs = (P("col", "row"), P())
    return jax.shard_map(body, mesh=mesh, in_specs=in_specs, out_specs=out_specs, check_vma=False)
```
